256 devices in a mesh: dp: 4 (over y), shard: 64 (over x, z, core).
Axes of the slice: x: 4, y: 4, z: 8, core: 2. Of those that a mesh axis runs over, the one named last changes fastest.
Arguments:
- training_inputs: bfloat16 [32768, 8192], P(('dp', 'shard')), may hold values from -6 to 6
- training_cotangents: bfloat16 [32768, 8192], P(('dp', 'shard')), may hold values from -6 to 6
- validation_inputs: bfloat16 [8192, 8192], P(('dp', 'shard')), may hold values from -6 to 6
- validation_cotangents: bfloat16 [8192, 8192], P(('dp', 'shard')), may hold values from -6 to 6
- adapter_down: bfloat16 [8192, 64], replicated, may hold values from -0.0625 to 0.0625
- adapter_up: bfloat16 [64, 8192], replicated, may hold values from -0.0625 to 0.0625
- adam_first_moment: bfloat16 [64, 128, 128], P('shard'), may hold values from -6 to 6
- adam_second_moment: bfloat16 [64, 128, 128], P('shard'), may hold values from 0.019897461 to 20
- slot_block_index: int32 [64], replicated, may hold values from 0 to 63, each once
- example_lengths: int32 [4, 64, 8], P('dp', 'shard'), may hold values from 1 to 64, 128 in all within a row
- projection_rows: float32 [128, 64], replicated, may hold values from -0.5 to 0.5
- projection_columns: float32 [8192, 128], replicated, may hold values from -0.0625 to 0.0625
Outputs:
- train_dirs: float32 [4, 64, 8, 8192], P('dp', 'shard')
- val_dir: float32 [8192], replicated
- scores: float32 [4, 64, 8], P('dp', 'shard')
The draws below stay inside these ranges and needn't reach their ends.
Inputs may be any that keep to these rules, and one draw needn't show every extreme that they name: slot_block_index holds every block number once. `example_lengths`: each device's 8 lengths sum to 128; on every device the longest example has exactly 64 tokens.
All inputs are finite; a program needn't handle non-finite values.
Results may differ from the reference program's by a relative error of at most 0.015.
Values may be sent and summed in bfloat16 or wider, within the bound.
A program may use at most 192 MiB of HBM per device.

```python
import math
import jax
import jax.numpy as jnp
import numpy as np
from jax import lax

MODEL_WIDTH = 8192
ADAPTER_RANK = 64
K1 = 64
K2 = 128
TOKENS_DEVICE = 128
EXAMPLES_DEVICE = 8
BLOCKS = 64
W = 128
GROUPS = 4
SCORERS = 64
TOKENS = 32768
VAL_TOKENS = 8192


def block_scale(own_key, dims, cuts, smallest, top_value):
    def one(dim, shards_of):
        draws = jax.random.uniform(jax.random.fold_in(jax.random.fold_in(own_key, 6), dim), (shards_of,), jnp.float32, smallest / len(cuts), top_value / len(cuts))
        return jnp.repeat(jnp.exp(draws), dims[dim] // shards_of).reshape((-1,) + (1,) * (len(dims) - dim - 1))

    level = one(*cuts[0])
    for cut in cuts[1:]:
        level = level * one(*cut)
    return level


def profile(count, total, reach, lean):
    loads = [(1 << 20) // math.isqrt(rank ** lean) + 1 for rank in range(2, count + 1)]
    spare, holding = total - reach - (count - 1), [1] * (count - 1)
    while spare > 0:
        candidates = [i for i in range(count - 1) if holding[i] < reach]
        whole, left = sum([loads[i] for i in candidates]), spare
        for i in candidates:
            extra = min(reach - holding[i], max(1, left * loads[i] // whole), spare)
            holding[i] = holding[i] + extra
            spare = spare - extra
    return np.array([reach] + holding)


def uneven(own_key, number_of, total, reach, slope):
    if number_of == 2:
        one = jax.random.randint(own_key, (), max(1, total - reach), min(reach, total - 1) + 1)
        return jnp.stack([one, total - one])
    sizes = jnp.asarray(profile(number_of, total, reach, slope), jnp.int32)
    pairs = (number_of - 1) // 2
    source_of, sink = sizes[1:1 + 2 * pairs:2], sizes[2:2 + 2 * pairs:2]
    slack = jnp.minimum(source_of - 1, reach - sink)
    moved = jax.random.randint(jax.random.fold_in(own_key, 1), (pairs,), 0, 1 << 20) % (slack + 1)
    sizes = sizes.at[1:1 + 2 * pairs:2].set(source_of - moved).at[2:2 + 2 * pairs:2].set(sink + moved)
    return sizes[jax.random.permutation(jax.random.fold_in(own_key, 2), number_of)]


def gaussian(stream_key, extent, spread, limit, split=(), held_as=jnp.bfloat16):
    loudness = block_scale(stream_key, extent, split, -0.22, 0.18) if split else 1.0
    drawn = jax.random.normal(stream_key, extent, jnp.float32) * spread * loudness
    return jnp.minimum(jnp.maximum(drawn, -limit), limit).astype(held_as)


def setup_inputs(seed: int = 0) -> dict:
    arg_keys = jax.random.split(jax.random.key(seed), 13)
    return {
        "training_inputs": gaussian(arg_keys[0], (TOKENS, MODEL_WIDTH), 1.0, 6.0, ((0, 256),)),
        "training_cotangents": gaussian(arg_keys[1], (TOKENS, MODEL_WIDTH), 1.0, 6.0, ((0, 256),)),
        "validation_inputs": gaussian(arg_keys[2], (VAL_TOKENS, MODEL_WIDTH), 1.0, 6.0, ((0, 256),)),
        "validation_cotangents": gaussian(arg_keys[3], (VAL_TOKENS, MODEL_WIDTH), 1.0, 6.0, ((0, 256),)),
        "adapter_down": gaussian(arg_keys[4], (MODEL_WIDTH, ADAPTER_RANK), MODEL_WIDTH ** -0.5, 0.0625),
        "adapter_up": gaussian(arg_keys[5], (ADAPTER_RANK, MODEL_WIDTH), MODEL_WIDTH ** -0.5, 0.0625),
        "adam_first_moment": gaussian(arg_keys[6], (BLOCKS, 2 * ADAPTER_RANK, W), 1.0, 6.0, ((0, 64),)),
        "adam_second_moment": jnp.clip(jnp.exp(math.log(20.0) - 6.912895 * jax.random.uniform(arg_keys[7], (BLOCKS, 2 * ADAPTER_RANK, W), jnp.float32) ** block_scale(arg_keys[7], (BLOCKS, 2 * ADAPTER_RANK, W), ((0, 64),), -0.2, 0.2)), 0.019897461, 20.0).astype(jnp.bfloat16),
        "slot_block_index": jax.random.permutation(arg_keys[8], BLOCKS).astype(jnp.int32),
        "example_lengths": jax.vmap(lambda own: uneven(own, EXAMPLES_DEVICE, TOKENS_DEVICE, TOKENS_DEVICE // 2, 2))(jax.random.split(arg_keys[9], GROUPS * SCORERS)).reshape((GROUPS, SCORERS, EXAMPLES_DEVICE)).astype(jnp.int32),
        "projection_rows": gaussian(arg_keys[10], (2 * ADAPTER_RANK, K1), (2 * ADAPTER_RANK) ** -0.5, 0.5, (), jnp.float32),
        "projection_columns": gaussian(arg_keys[11], (MODEL_WIDTH, K2), MODEL_WIDTH ** -0.5, 0.0625, (), jnp.float32),
    }


beta_first = 0.9
beta_second = 0.999
epsilon = 1e-06

def membership(lengths, total_rows):
    finish = jnp.cumsum(lengths)
    begins = finish - lengths
    position = jnp.arange(total_rows, dtype=jnp.int32)[:, None]
    return ((position >= begins[None, :]) & (position < finish[None, :])).astype(jnp.bfloat16)

def reduced_rank(input_rows, output_cotangent, adapter_down, adapter_up):
    backward_adapter = jnp.dot(output_cotangent, adapter_up.T, preferred_element_type=jnp.float32).astype(jnp.bfloat16)
    forward_adapter = jnp.dot(input_rows, adapter_down, preferred_element_type=jnp.float32).astype(jnp.bfloat16)
    return (backward_adapter, forward_adapter)

def normalize(vector):
    return vector / jnp.sqrt(lax.optimization_barrier(jnp.mean(vector * vector, axis=-1, keepdims=True)) + epsilon)

def project(gradient, projection_rows, columns):
    inner = jnp.dot(gradient, columns, precision=lax.Precision.HIGHEST)
    return jnp.einsum('rj,rk->jk', projection_rows, inner, precision=lax.Precision.HIGHEST)

def reference(training_inputs, training_cotangents, validation_inputs, validation_cotangents, adapter_down, adapter_up, adam_first_moment, adam_second_moment, slot_block_index, example_lengths, projection_rows, projection_columns):
    adapter_rank = adapter_down.shape[1]
    sorted_first_moment = jnp.zeros_like(adam_first_moment).at[slot_block_index].set(adam_first_moment)
    sorted_second_moment = jnp.zeros_like(adam_second_moment).at[slot_block_index].set(adam_second_moment)
    moment_first_slot = sorted_first_moment.astype(jnp.float32).transpose(1, 0, 2).reshape(2 * adapter_rank, MODEL_WIDTH)
    moment_second_slot = sorted_second_moment.astype(jnp.float32).transpose(1, 0, 2).reshape(2 * adapter_rank, MODEL_WIDTH)
    validation_backward, validation_forward = reduced_rank(validation_inputs, validation_cotangents, adapter_down, adapter_up)
    val_grad = jnp.concatenate([jnp.dot(validation_backward.T, validation_inputs, preferred_element_type=jnp.float32), jnp.dot(validation_forward.T, validation_cotangents, preferred_element_type=jnp.float32)], axis=0)
    val_dir = normalize(project(val_grad, projection_rows, projection_columns).reshape(K1 * K2))
    inputs_all = training_inputs.reshape(GROUPS * SCORERS, TOKENS_DEVICE, MODEL_WIDTH)
    cotangent_all = training_cotangents.reshape(GROUPS * SCORERS, TOKENS_DEVICE, MODEL_WIDTH)
    lengths_all = example_lengths.reshape(GROUPS * SCORERS, EXAMPLES_DEVICE)

    def one_device(packed):
        input_rows, output_cotangent, lengths = packed
        backward_adapter, forward_adapter = reduced_rank(input_rows, output_cotangent, adapter_down, adapter_up)
        member_flag = membership(lengths, TOKENS_DEVICE)
        masked_backward = (backward_adapter[:, None, :] * member_flag[:, :, None]).reshape(TOKENS_DEVICE, EXAMPLES_DEVICE * adapter_rank)
        forward_masked = (forward_adapter[:, None, :] * member_flag[:, :, None]).reshape(TOKENS_DEVICE, EXAMPLES_DEVICE * adapter_rank)
        top_half = jnp.dot(masked_backward.T, input_rows, preferred_element_type=jnp.float32).reshape(EXAMPLES_DEVICE, adapter_rank, MODEL_WIDTH)
        bottom_half = jnp.dot(forward_masked.T, output_cotangent, preferred_element_type=jnp.float32).reshape(EXAMPLES_DEVICE, adapter_rank, MODEL_WIDTH)
        gradient = jnp.concatenate([top_half, bottom_half], axis=1)
        update = (beta_first * moment_first_slot[None] + (1 - beta_first) * gradient) / jnp.sqrt(beta_second * moment_second_slot[None] + (1 - beta_second) * gradient * gradient)
        inner = jnp.einsum('erd,dk->erk', update, projection_columns, precision=lax.Precision.HIGHEST)
        projected = jnp.einsum('rj,erk->ejk', projection_rows, inner, precision=lax.Precision.HIGHEST)
        return normalize(projected.reshape(EXAMPLES_DEVICE, K1 * K2))
    directions = lax.map(one_device, (inputs_all, cotangent_all, lengths_all))
    directions = directions.reshape(GROUPS, SCORERS, EXAMPLES_DEVICE, K1 * K2)
    scores = lax.optimization_barrier(jnp.sum(directions * val_dir, axis=-1)) / math.sqrt(K1 * K2)
    return (directions, val_dir, scores)
```

```python
import math

import jax
import jax.numpy as jnp
from jax import lax
from jax.experimental import pallas as pl
from jax.experimental.pallas import tpu as pltpu
from jax.sharding import PartitionSpec as P

NX, NY, NZ = 4, 4, 8
SLOTS = 2 * NX * NZ
PAIRS = SLOTS // 2
LEAD = 9
W = 128
RANK = 64
EXAMPLES = 8
WIDTH = 8192
TOKENS = 128
VAL = 32
CHUNK = 1024

beta_first = 0.9
beta_second = 0.999
epsilon = 1e-06
FIRST = beta_first / (1 - beta_first)
SECOND = beta_second / (1 - beta_second)
GAIN = (1 - beta_first) / math.sqrt(1 - beta_second)

MESH = pl.DeviceIdType.MESH
HIGHEST = lax.Precision.HIGHEST


def offset(i):
    return ((i + 1) // 2) * (1 - 2 * (i % 2))


def even_order(k):
    late = (k >= 8).astype(jnp.int32)
    last = (k >= 24).astype(jnp.int32)
    g = late * (1 - last) * (1 + k % 2) + last * 3
    j = (1 - late) * k + late * (1 - last) * ((k - 8) // 2) + last * (k - 24)
    return g, j


def odd_order(k):
    late = (k >= 4).astype(jnp.int32)
    last = (k >= 28).astype(jnp.int32)
    hop = 1 + (k - 4) // 8
    i = (k + 4) % 8
    g = (1 - late) * k + late * (1 - last) * (i // 2) + last * (k - 28)
    j = late * (1 - last) * (2 * hop - 1 + i % 2) + last * 7
    return g, j


def split(a):
    high = a.astype(jnp.bfloat16)
    return high, (a - high.astype(jnp.float32)).astype(jnp.bfloat16)


def nt(a, b):
    return lax.dot_general(a, b, (((1,), (1,)), ((), ())), preferred_element_type=jnp.float32)


def prepare(
    x_hbm, ct_hbm, xv_hbm, ctv_hbm, down_hbm, up_hbm, pc_hbm, rt_ref, blocks, lengths,
    x_slots, ct_slots, table_slots, masked, val_part,
    xs, cts, xvs, ctvs, downs, ups, pcs, load_sem,
):
    loads = [
        pltpu.make_async_copy(a, b, load_sem.at[i])
        for i, (a, b) in enumerate(
            [(up_hbm, ups), (ct_hbm, cts), (down_hbm, downs), (x_hbm, xs), (pc_hbm, pcs), (xv_hbm, xvs), (ctv_hbm, ctvs)]
        )
    ]
    for copy in loads:
        copy.start()

    def reduced(weights, rows, count):
        def step(i, total_):
            cols = pl.ds(pl.multiple_of(i * CHUNK, CHUNK), CHUNK)
            return total_ + nt(weights[:, cols], rows[:, cols])

        return lax.fori_loop(0, WIDTH // CHUNK, step, jnp.zeros((RANK, count), jnp.float32)).astype(jnp.bfloat16)

    lane = lax.broadcasted_iota(jnp.int32, (RANK, TOKENS), 1)

    def mask(half, adapted):
        begin = jnp.int32(0)
        for e in range(EXAMPLES):
            finish = begin + lengths[e]
            inside = (lane >= begin) & (lane < finish)
            masked[half, e * RANK : (e + 1) * RANK, :] = jnp.where(inside, adapted.astype(jnp.float32), 0.0).astype(jnp.bfloat16)
            begin = finish

    loads[0].wait()
    loads[1].wait()
    mask(0, reduced(ups, cts, TOKENS))
    loads[2].wait()
    loads[3].wait()
    mask(1, reduced(downs, xs, TOKENS))
    for i in (4, 5, 6):
        loads[i].wait()
    vback = reduced(ups, ctvs, VAL)
    vfwd = reduced(downs, xvs, VAL)

    def val_step(i, carry):
        a, b = carry
        cols = pl.ds(pl.multiple_of(i * CHUNK, CHUNK), CHUNK)
        for part in split(pcs[cols, :]):
            a = a + jnp.dot(xvs[:, cols], part, preferred_element_type=jnp.float32)
            b = b + jnp.dot(ctvs[:, cols], part, preferred_element_type=jnp.float32)
        return a, b

    zero = jnp.zeros((VAL, W), jnp.float32)
    in_cols, ct_cols = lax.fori_loop(0, WIDTH // CHUNK, val_step, (zero, zero))
    val_inner = jnp.concatenate(
        [
            jnp.dot(vback.astype(jnp.float32), in_cols, precision=HIGHEST, preferred_element_type=jnp.float32),
            jnp.dot(vfwd.astype(jnp.float32), ct_cols, precision=HIGHEST, preferred_element_type=jnp.float32),
        ],
        axis=0,
    )
    val_part[...] = jnp.dot(rt_ref[...], val_inner, precision=HIGHEST, preferred_element_type=jnp.float32)

    def reorder(i, _):
        for j in range(4):
            slot = 4 * i + j
            columns = pl.ds(pl.multiple_of(blocks[slot] * W, W), W)
            x_slots[slot] = xs[:, columns]
            ct_slots[slot] = cts[:, columns]
            for i_part, part in enumerate(split(pcs[columns, :])):
                table_slots[slot, i_part] = part
        return 0

    lax.fori_loop(0, SLOTS // 4, reorder, 0)


def kernel(
    m_hbm, v_hbm, x_slots, ct_slots, table_slots, masked, val_part, rt_ref,
    dirs_ref, vdir_ref, scores_ref,
    mom, acc, red_c, red_y, red_x, red_z,
    own_sem, recv, send, rc_recv, ry_recv, rx_recv, rz_recv, rc_send, ry_send, rx_send, rz_send,
):
    me = lax.axis_index("shard")
    my_y = lax.axis_index("dp")
    core = me % 2
    my_z = (me // 2) % NZ
    my_x = me // (2 * NZ)

    def place(x, z, c):
        return (x * NZ + z) * 2 + c

    partner = place(my_x, my_z, 1 - core)

    own_copies = [
        pltpu.make_async_copy(m_hbm.at[0], mom.at[me, 0], own_sem.at[0]),
        pltpu.make_async_copy(v_hbm.at[0], mom.at[me, 1], own_sem.at[1]),
    ]
    barrier = pltpu.get_barrier_semaphore()

    def greet(axis, peer):
        pl.semaphore_signal(barrier, inc=1, device_id={axis: peer}, device_id_type=MESH)

    for d in range(1, NZ):
        greet("shard", place(my_x, (my_z + d) % NZ, core))
    for d in range(1, NX):
        greet("shard", place((my_x + d) % NX, my_z, core))
    for d in range(1, NY):
        greet("dp", (my_y + d) % NY)
    greet("shard", partner)
    for copy in own_copies:
        copy.start()
    for copy in own_copies:
        copy.wait()
    pl.semaphore_wait(barrier, NZ + NX + NY - 3 + 1)

    def slot_copy(slot, k, way, peer):
        return pltpu.make_async_remote_copy(
            src_ref=mom.at[slot],
            dst_ref=mom.at[slot],
            send_sem=send.at[k, way],
            recv_sem=recv.at[slot],
            device_id={"shard": peer},
            device_id_type=MESH,
        )

    def even_slot(k):
        g, j = even_order(k)
        return place((my_x + offset(g) + NX) % NX, (my_z + offset(j) + NZ) % NZ, 0)

    def odd_slot(k):
        g, j = odd_order(k)
        return place((my_x + offset(g) + NX) % NX, (my_z + offset(j) + NZ) % NZ, 1)

    def sends(k, act):
        x_up, x_down = place((my_x + 1) % NX, my_z, core), place((my_x + NX - 1) % NX, my_z, core)
        z_up, z_down = place(my_x, (my_z + 1) % NZ, core), place(my_x, (my_z + NZ - 1) % NZ, core)

        def go(cond, slot, way, peer):
            @pl.when(cond)
            def _():
                act(slot_copy(slot, k, way, peer))

        @pl.when(core == 0)
        def _():
            slot = even_slot(k)
            first, second = k < 8, (k >= 8) & (k < 24)
            g, j = even_order(k)
            go(first & ((k == 0) | ((k % 2 == 1) & (k <= 5))), slot, 0, z_up)
            go(first & ((k % 2 == 0) & (k <= 4)), slot, 1, z_down)
            go(first | (second & (g == 1) & (j % 2 == 0)), slot, 2, x_up)
            go(first | (second & (g == 2) & (j % 2 == 1)), slot, 3, x_down)
            act(slot_copy(slot, k, 4, partner))

        @pl.when(core == 1)
        def _():
            slot = odd_slot(k)
            first, second = k < 4, (k >= 4) & (k < 28)
            g, j = odd_order(k)
            go(first | (second & (j % 2 == 1) & ((j <= 3) | (g % 2 == 0))), slot, 0, z_up)
            go(first | (second & (j % 2 == 0) & ((j <= 4) | (g % 2 == 1))), slot, 1, z_down)
            go(first & (k <= 1), slot, 2, x_up)
            go(k == 0, slot, 3, x_down)
            act(slot_copy(slot, k, 4, partner))

    def arrive(k):
        slot = (1 - core) * even_slot(k) + core * odd_slot(k)
        slot_copy(slot, k, 4, partner).wait_recv()
        sends(k, lambda copy: copy.start())

    def spread(buffer, mine, peers, send_sems, recv_sems, axis, act):
        for i, (peer, theirs) in enumerate(peers):
            source = theirs if act == "wait" else mine
            copy = pltpu.make_async_remote_copy(
                src_ref=buffer.at[source],
                dst_ref=buffer.at[source],
                send_sem=send_sems.at[i],
                recv_sem=recv_sems.at[source],
                device_id={axis: peer},
                device_id_type=MESH,
            )
            if act == "start":
                copy.start()
            elif act == "sent":
                copy.wait_send()
            else:
                copy.wait_recv()

    def stage(name, act):
        if name == "core":
            spread(red_c, core, [(partner, 1 - core)], rc_send, rc_recv, "shard", act)
        elif name == "y":
            there = [(my_y + d) % NY for d in range(1, NY)]
            spread(red_y, my_y, [(t, t) for t in there], ry_send, ry_recv, "dp", act)
        elif name == "x":
            there = [(my_x + d) % NX for d in range(1, NX)]
            spread(red_x, my_x, [(place(t, my_z, core), t) for t in there], rx_send, rx_recv, "shard", act)
        else:
            there = [(my_z + d) % NZ for d in range(1, NZ)]
            spread(red_z, my_z, [(place(my_x, t, core), t) for t in there], rz_send, rz_recv, "shard", act)

    def total(buffer, count):
        out = buffer[0]
        for i in range(1, count):
            out = out + buffer[i]
        return out

    const = lambda i: jnp.int32(i)
    sends(const(0), lambda copy: copy.start())

    red_c[core] = val_part[...]
    acc[...] = jnp.zeros_like(acc)

    def pair(k, _):
        @pl.when(k < LEAD - 1)
        def _():
            arrive(2 * k + 1)
            arrive(2 * k + 2)

        @pl.when((k >= LEAD - 1) & (k < PAIRS - LEAD))
        def _():
            arrive(k + LEAD)

        @pl.when(k == 0)
        def _():
            stage("core", "start")

        @pl.when(k == 2)
        def _():
            stage("core", "wait")
            red_y[my_y] = total(red_c, 2)

        @pl.when(k == 3)
        def _():
            stage("y", "start")

        @pl.when(k == 7)
        def _():
            stage("y", "wait")
            red_x[my_x] = total(red_y, NY)

        @pl.when(k == 8)
        def _():
            stage("x", "start")

        @pl.when(k == 12)
        def _():
            stage("x", "wait")
            red_z[my_z] = total(red_x, NX)

        @pl.when(k == 13)
        def _():
            stage("z", "start")

        slots = [even_slot(k), odd_slot(k)]
        theirs = core * slots[0] + (1 - core) * slots[1]
        slot_copy(theirs, k, 4, partner).wait_recv()
        table = jnp.concatenate([table_slots[s, part] for part in range(2) for s in slots], axis=0)
        for half, rows in ((0, x_slots), (1, ct_slots)):
            right = jnp.concatenate([rows[s] for s in slots], axis=1)
            grad = jnp.dot(masked[half], right, preferred_element_type=jnp.float32)
            span = slice(half * RANK, (half + 1) * RANK)
            first = FIRST * jnp.concatenate([mom[s, 0, span, :] for s in slots], axis=1).astype(jnp.float32)
            second = SECOND * jnp.concatenate([mom[s, 1, span, :] for s in slots], axis=1).astype(jnp.float32)
            parts = []
            for e in range(EXAMPLES):
                g = grad[e * RANK : (e + 1) * RANK]
                parts.append(((first + g) * lax.rsqrt(second + g * g)).astype(jnp.bfloat16))
            update = jnp.concatenate(parts, axis=0)
            acc[half] += jnp.dot(jnp.concatenate([update, update], axis=1), table, preferred_element_type=jnp.float32)
        return 0

    lax.fori_loop(0, PAIRS, pair, 0)

    stage("z", "wait")
    val_proj = total(red_z, NZ)
    val_dir = val_proj / jnp.sqrt(jnp.sum(val_proj * val_proj, keepdims=True) / (RANK * W) + epsilon)
    vdir_ref[...] = val_dir
    where = lax.broadcasted_iota(jnp.int32, (1, EXAMPLES), 1)
    scores = jnp.zeros((1, EXAMPLES), jnp.float32)
    for e in range(EXAMPLES):
        rows = slice(e * RANK, (e + 1) * RANK)
        inner = jnp.concatenate([acc[0, rows, :], acc[1, rows, :]], axis=0)
        proj = GAIN * jnp.dot(rt_ref[...], inner, precision=HIGHEST, preferred_element_type=jnp.float32)
        direction = proj / jnp.sqrt(jnp.sum(proj * proj, keepdims=True) / (RANK * W) + epsilon)
        dirs_ref[pl.ds(e, RANK, stride=EXAMPLES), :] = direction
        score = jnp.sum(direction * val_dir, keepdims=True) / math.sqrt(RANK * W)
        scores = scores + jnp.where(where == e, score, 0.0)
    scores_ref[...] = scores

    for name in ("core", "y", "x", "z"):
        stage(name, "sent")

    def drain(k, _):
        sends(k, lambda copy: copy.wait_send())
        return 0

    lax.fori_loop(0, PAIRS, drain, 0)


def body(
    training_inputs,
    training_cotangents,
    validation_inputs,
    validation_cotangents,
    adapter_down,
    adapter_up,
    adam_first_moment,
    adam_second_moment,
    slot_block_index,
    example_lengths,
    projection_rows,
    projection_columns,
):
    hbm = pl.BlockSpec(memory_space=pltpu.MemorySpace.HBM)
    vmem = pl.BlockSpec(memory_space=pltpu.MemorySpace.VMEM)
    smem = pl.BlockSpec(memory_space=pltpu.MemorySpace.SMEM)
    bf16, f32 = jnp.bfloat16, jnp.float32
    dma = pltpu.SemaphoreType.DMA
    rows_t = projection_rows.T
    slots = jax.ShapeDtypeStruct((SLOTS, W, W), bf16)
    x_slots, ct_slots, table_slots, masked, val_part = pl.pallas_call(
        prepare,
        name="prepare",
        out_shape=(
            slots,
            slots,
            jax.ShapeDtypeStruct((SLOTS, 2, W, W), bf16),
            jax.ShapeDtypeStruct((2, EXAMPLES * RANK, TOKENS), bf16),
            jax.ShapeDtypeStruct((RANK, W), f32),
        ),
        in_specs=[hbm] * 7 + [vmem, smem, smem],
        out_specs=(vmem,) * 5,
        scratch_shapes=[
            pltpu.VMEM((TOKENS, WIDTH), bf16),
            pltpu.VMEM((TOKENS, WIDTH), bf16),
            pltpu.VMEM((VAL, WIDTH), bf16),
            pltpu.VMEM((VAL, WIDTH), bf16),
            pltpu.VMEM((RANK, WIDTH), bf16),
            pltpu.VMEM((RANK, WIDTH), bf16),
            pltpu.VMEM((WIDTH, W), f32),
            dma((7,)),
        ],
        compiler_params=pltpu.CompilerParams(vmem_limit_bytes=36 * 1024 * 1024),
    )(
        training_inputs,
        training_cotangents,
        validation_inputs,
        validation_cotangents,
        adapter_down.T,
        adapter_up,
        projection_columns,
        rows_t,
        slot_block_index,
        example_lengths.reshape(EXAMPLES),
    )
    dirs, val_dir, scores = pl.pallas_call(
        kernel,
        name="influence",
        out_shape=(
            jax.ShapeDtypeStruct((EXAMPLES * RANK, W), f32),
            jax.ShapeDtypeStruct((RANK, W), f32),
            jax.ShapeDtypeStruct((1, EXAMPLES), f32),
        ),
        in_specs=[hbm] * 2 + [vmem] * 6,
        out_specs=(vmem, vmem, vmem),
        scratch_shapes=[
            pltpu.VMEM((SLOTS, 2, W, W), bf16),
            pltpu.VMEM((2, EXAMPLES * RANK, W), f32),
            pltpu.VMEM((2, RANK, W), f32),
            pltpu.VMEM((NY, RANK, W), f32),
            pltpu.VMEM((NX, RANK, W), f32),
            pltpu.VMEM((NZ, RANK, W), f32),
            dma((2,)),
            dma((SLOTS,)),
            dma((PAIRS, 5)),
            dma((2,)),
            dma((NY,)),
            dma((NX,)),
            dma((NZ,)),
            dma((1,)),
            dma((NY - 1,)),
            dma((NX - 1,)),
            dma((NZ - 1,)),
        ],
        compiler_params=pltpu.CompilerParams(
            collective_id=0, has_side_effects=True, vmem_limit_bytes=32 * 1024 * 1024
        ),
    )(adam_first_moment, adam_second_moment, x_slots, ct_slots, table_slots, masked, val_part, rows_t)
    dirs = dirs.reshape(RANK, EXAMPLES, W).transpose(1, 0, 2).reshape(1, 1, EXAMPLES, RANK * W)
    return (dirs, val_dir.reshape(RANK * W), scores.reshape(1, 1, EXAMPLES))


def solution(mesh):
    return jax.shard_map(
        body,
        mesh=mesh,
        in_specs=(
            P(("dp", "shard"), None),
            P(("dp", "shard"), None),
            P(("dp", "shard"), None),
            P(("dp", "shard"), None),
            P(),
            P(),
            P("shard", None, None),
            P("shard", None, None),
            P(),
            P("dp", "shard", None),
            P(),
            P(),
        ),
        out_specs=(P("dp", "shard", None, None), P(), P("dp", "shard", None)),
        check_vma=False,
    )
```
